128 devices in a mesh: gx: 16 (over z_hi, y, core), gy: 8 (over z_lo, x).
Axes of the slice: x: 4, y: 4, z: 4 (z_hi: 2, z_lo: 2; z = z_hi * 2 + z_lo), core: 2. Of those that a mesh axis runs over, the one named last changes fastest.
Arguments:
- resid_factor: float32 [8, 128, 128, 512], P(None, 'gx', 'gy'), may hold values from -8 to 8
- coefficients: float32 [6, 128, 128, 512], P(None, 'gx', 'gy'), may hold values from 0.2 to 2
- observer: bfloat16 [128, 128, 128, 512], P(None, 'gx', 'gy'), may hold values from -0.001953125 to 0.001953125
- shift_index: int32 [8], replicated, may hold values from 0 to 15
Outputs:
- factor: float32 [8, 128, 128, 512], P(None, 'gx', 'gy')
- new_resid: float32 [8, 128, 128, 512], P(None, 'gx', 'gy')
- gram: float32 [8, 128], replicated
- norms: float32 [8], replicated
The draws below stay inside these ranges and needn't reach their ends.
All inputs are finite; a program needn't handle non-finite values.
Results may differ from the reference program's by a relative error of at most 0.0029.
Values sent between devices are 32-bit elements; how exact they have to be, the bound alone decides.
No kernel may reach another device: no remote copies, remote signals or barrier semaphores. Data moves between devices by JAX's collectives and lax.ppermute only.
A program may use at most 128 MiB of HBM per device.

```python
import math
import jax
import jax.numpy as jnp
from jax import lax

NZ = 512
COLS = 8
QCOLS = 128
NX = 128
NY = 128


def draw_resid_factor(key, part):
    shape = (COLS, NX, NY, NZ)
    first_key, second_key = jax.random.split(jax.random.fold_in(key, 11))
    xpos = lax.broadcasted_iota(jnp.float32, shape, 1)
    rising = jnp.exp(jnp.log(3.0) * xpos / NX)
    rough = jnp.clip(jax.random.normal(first_key, shape, jnp.float32), -4.0, 4.0)
    scales = jnp.exp(jax.random.uniform(second_key, shape, jnp.float32, -0.35, 0.35))
    values = 0.6 * rising * rough * scales
    return jnp.clip(values, -8.0, 8.0).astype(jnp.float32)


def plant(drawn, stream_key, least, high):
    place = [jax.random.randint(jax.random.fold_in(stream_key, axis), (), 0, length) for axis, length in enumerate(drawn.shape)]
    main_axis = drawn.shape.index(max(drawn.shape))
    next_to = place[:main_axis] + [(place[main_axis] + 1) % drawn.shape[main_axis]] + place[main_axis + 1:]
    return drawn.at[tuple(place)].set(least).at[tuple(next_to)].set(high)


def block_levels(own_key, extent, cuts, low, top_value):
    def one(dim, parts):
        heights = jax.random.uniform(jax.random.fold_in(jax.random.fold_in(own_key, 6), dim), (parts,), jnp.float32, low / len(cuts), top_value / len(cuts))
        return jnp.repeat(jnp.exp(heights), extent[dim] // parts).reshape((-1,) + (1,) * (len(extent) - dim - 1))

    factor_of = one(*cuts[0])
    for cut in cuts[1:]:
        factor_of = factor_of * one(*cut)
    return factor_of


def normal_values(own_key, extent, width, reach, pieces=(), kind=jnp.bfloat16):
    factor_of = block_levels(own_key, extent, pieces, -0.22, 0.18) if pieces else 1.0
    drawn = jax.random.normal(own_key, extent, jnp.float32) * width * factor_of
    return jnp.minimum(jnp.maximum(drawn, -reach), reach).astype(kind)


def setup_inputs(seed: int = 0) -> dict:
    key_of = jax.random.split(jax.random.key(seed), 5)
    return {
        "resid_factor": draw_resid_factor(jax.random.fold_in(key_of[4], 71), 0),
        "coefficients": jnp.clip(jnp.exp(math.log(2.0) - 2.3025851 * jax.random.uniform(key_of[1], (6, NX, NY, NZ), jnp.float32) ** block_levels(key_of[1], (6, NX, NY, NZ), ((1, 16), (2, 8)), -0.2, 0.2)), 0.2, 2.0),
        "observer": normal_values(key_of[2], (QCOLS, NX, NY, NZ), (NX * NY * NZ) ** -0.5, 0.001953125, ((1, 16), (2, 8))),
        "shift_index": plant(jax.random.randint(key_of[3], (COLS,), 0, 16), jax.random.fold_in(key_of[3], 1), 0, 15).astype(jnp.int32),
    }


def shift_values(shift_index):
    return 0.2 * jnp.exp(jnp.log(40.0) * shift_index.astype(jnp.float32) / 15.0)

def neighbour_sum(field, coefficients):
    zpadded = jnp.pad(field, ((0, 0), (0, 0), (0, 0), (1, 1)))
    total = coefficients[0] * jnp.roll(field, 1, axis=1) + coefficients[1] * jnp.roll(field, -1, axis=1)
    total = total + coefficients[2] * jnp.roll(field, 1, axis=2) + coefficients[3] * jnp.roll(field, -1, axis=2)
    total = total + coefficients[4] * zpadded[..., :-2] + coefficients[5] * zpadded[..., 2:]
    return total

def reference(resid_factor, coefficients, observer, shift_index):
    sigma = shift_values(shift_index)[:, None, None, None]
    radius = 12.0 / (12.0 + sigma)
    omega_two = 1.0 / (1.0 - radius * radius / 2.0)
    omega_three = 1.0 / (1.0 - radius * radius * omega_two / 4.0)
    diagonal = lax.optimization_barrier(jnp.sum(coefficients, axis=0))[None] + sigma

    def jacobi(field):
        return (resid_factor + neighbour_sum(field, coefficients)) / diagonal
    start = resid_factor / diagonal
    second = jacobi(start)
    third = start + omega_two * (jacobi(second) - start)
    solved = second + omega_three * (jacobi(third) - second)
    factor = jnp.sqrt(2.0 * sigma) * solved
    new_resid = resid_factor - 2.0 * sigma * solved
    flat = factor.astype(jnp.bfloat16).reshape(COLS, -1)
    gram = lax.dot_general(flat, observer.reshape(QCOLS, -1), (((1,), (1,)), ((), ())), preferred_element_type=jnp.float32)
    norms = lax.optimization_barrier(jnp.sum(new_resid * new_resid, axis=(1, 2, 3))) / (NX * NY * NZ)
    return (factor, new_resid, gram, norms)
```

```python
import jax
import jax.numpy as jnp
from jax import lax
from jax.experimental import pallas as pl
from jax.experimental.pallas import tpu as pltpu
from jax.sharding import Mesh, PartitionSpec as P

COLS = 8
QCOLS = 128
LX = 8
LY = 16
CELLS = LX * LY
NZ = 512
ZT = NZ // 128
STEP = CELLS * ZT
F32 = jnp.float32
BF16 = jnp.bfloat16

GX = ("zh", "y", "core")
GY = ("zl", "x")
CHIPS = ("zh", "y", "zl", "x")

VM = pl.BlockSpec(memory_space=pltpu.VMEM)
HB = pl.BlockSpec(memory_space=pltpu.HBM)
SM = pl.BlockSpec(memory_space=pltpu.SMEM)

FIELD = (CELLS, COLS, NZ)
XFACE = (LY, COLS, NZ)
YFACE = (LX, COLS, NZ)


def sds(shape, dtype=F32):
    return jax.ShapeDtypeStruct(shape, dtype)


def stored(block):
    n = block.shape[0]
    return block.reshape(n, LX, LY // 8, 8, ZT, 128).transpose(0, 1, 2, 4, 3, 5).reshape(n * STEP, 128)


def unstored(rows):
    n = rows.shape[0] // STEP
    return rows.reshape(n, LX, LY // 8, ZT, 8, 128).transpose(0, 1, 2, 4, 3, 5).reshape(n, LX, LY, NZ)


def base(r):
    return (r // 8) * 32 + lax.rem(r, 8)


def spot(r):
    return r if isinstance(r, tuple) else (r // 8, lax.rem(r, 8))


def coef(c_ref, k, r):
    t, j = spot(r)
    at = k * STEP + t * 32 + j
    return jnp.concatenate([c_ref[pl.ds(at + zt * 8, COLS, stride=0), :] for zt in range(ZT)], axis=1)


def columns(r_ref, r):
    t, j = spot(r)
    at = t * 32 + j
    return jnp.concatenate([r_ref[pl.ds(at + zt * 8, COLS, stride=STEP), :] for zt in range(ZT)], axis=1)


def put_columns(o_ref, r, v):
    t, j = spot(r)
    at = t * 32 + j
    for zt in range(ZT):
        o_ref[pl.ds(at + zt * 8, COLS, stride=STEP), :] = v[:, zt * 128 : zt * 128 + 128]


def wide(v):
    return jnp.concatenate([v] * ZT, axis=1)


def x_row(high, i):
    return jnp.where(high, CELLS - LY, 0) + i


def y_row(high, i):
    return jnp.where(high, LY - 1, 0) + LY * i


def face_sides():
    even_x = lax.axis_index("core") == 0
    even_y = lax.rem(lax.axis_index("x"), 2) == 0
    return jnp.logical_not(even_x), jnp.logical_not(even_y), even_y, even_x


def first_kernel(shift_ref, r_hbm, c_hbm, sb, sd, sc, sa, prm, rs, cs, sem):
    get_c = pltpu.make_async_copy(c_hbm, cs, sem.at[0])
    get_r = pltpu.make_async_copy(r_hbm, rs, sem.at[1])
    get_c.start()
    get_r.start()
    row = lax.broadcasted_iota(jnp.int32, (COLS, 128), 0)
    index = jnp.zeros((COLS, 128), F32)
    for c in range(COLS):
        index = jnp.where(row == c, shift_ref[c].astype(F32), index)
    sigma = 0.2 * jnp.exp(jnp.log(jnp.full((COLS, 128), 40.0, F32)) * index / 15.0)
    radius = 12.0 / (12.0 + sigma)
    omega_two = 1.0 / (1.0 - radius * radius / 2.0)
    omega_three = 1.0 / (1.0 - radius * radius * omega_two / 4.0)
    prm[0] = sigma
    prm[1] = omega_two
    prm[2] = omega_three
    prm[3] = jnp.sqrt(2.0 * sigma)
    prm[4] = 2.0 * sigma
    fb, fd, fc, fa = face_sides()
    sigma = wide(sigma)
    get_c.wait()
    get_r.wait()

    def start_of(r):
        d = coef(cs, 0, r)
        for k in range(1, 6):
            d = d + coef(cs, k, r)
        return columns(rs, r) / (d + sigma)

    tb, ta = jnp.where(fb, CELLS // 8 - 2, 0), jnp.where(fa, CELLS // 8 - 2, 0)
    for j in range(8):
        for half in range(2):
            sb[half * 8 + j] = start_of((tb + half, j))
            sa[half * 8 + j] = start_of((ta + half, j))

    def ys(i, _):
        sd[i] = start_of(y_row(fd, i))
        sc[i] = start_of(y_row(fc, i))
        return 0

    lax.fori_loop(0, LX, ys, 0, unroll=4)


def spread(f_ref, cz, t, j):
    r = 8 * t + j
    v = f_ref[r]
    below = jnp.maximum(r - 1, 0) if j == 0 else r - 1
    above = jnp.minimum(r + 1, CELLS - 1) if j == 7 else r + 1
    total = coef(cz, 4, (t, j)) * pltpu.roll(v, 1, 1)
    total += coef(cz, 5, (t, j)) * pltpu.roll(v, NZ - 1, 1)
    total += coef(cz, 0, (t, j)) * f_ref[8 * jnp.maximum(t - 2, 0) + j]
    total += coef(cz, 1, (t, j)) * f_ref[8 * jnp.minimum(t + 2, CELLS // 8 - 1) + j]
    total += coef(cz, 2, (t, j)) * f_ref[below]
    total += coef(cz, 3, (t, j)) * f_ref[above]
    return total


def second_kernel(rs, cs, prm, o_hbm, start, rdiag, resid, cz, part, ov, sem):
    load = pltpu.make_async_copy(o_hbm, ov, sem)
    load.start()
    sigma = wide(prm[0])
    row = lax.broadcasted_iota(jnp.int32, (64, 128), 0)
    lane = lax.broadcasted_iota(jnp.int32, (64, 128), 1)
    in32, in8 = lax.rem(row, 32), lax.rem(row, 8)
    outside = (
        None,
        None,
        jnp.logical_and(row < 32, in8 == 0),
        jnp.logical_and(row >= 32, in8 == 7),
        jnp.logical_and(in32 < 8, lane == 0),
        jnp.logical_and(in32 >= 24, lane == 127),
    )
    for k in range(6):
        for x in range(LX):
            rows = pl.ds(k * STEP + x * 64, 64)
            if (k, x) in ((0, 0), (1, LX - 1)):
                cz[rows, :] = jnp.zeros((64, 128), F32)
            elif k < 2:
                cz[rows, :] = cs[rows, :]
            else:
                cz[rows, :] = jnp.where(outside[k], 0.0, cs[rows, :])

    def begin(t, _):
        for j in range(8):
            d = coef(cs, 0, (t, j))
            for k in range(1, 6):
                d = d + coef(cs, k, (t, j))
            recip = 1.0 / (d + sigma)
            res = columns(rs, (t, j))
            resid[8 * t + j] = res
            rdiag[8 * t + j] = recip
            start[8 * t + j] = res * recip
        return 0

    lax.fori_loop(0, CELLS // 8, begin, 0)

    def sweep(t, _):
        for j in range(8):
            r = 8 * t + j
            part[r] = (resid[r] + spread(start, cz, t, j)) * rdiag[r]
        return 0

    lax.fori_loop(0, CELLS // 8, sweep, 0)
    load.wait()


def third_kernel(field, before, resid, rdiag, cz, prm, part):
    omega = wide(prm[1])

    def sweep(t, _):
        for j in range(8):
            r = 8 * t + j
            s = before[r]
            part[r] = s + omega * ((resid[r] + spread(field, cz, t, j)) * rdiag[r] - s)
        return 0

    lax.fori_loop(0, CELLS // 8, sweep, 0)


def fourth_kernel(field, before, resid, rdiag, cz, prm, part, fscr, nscr, low, total):
    omega, root, twice = wide(prm[2]), wide(prm[3]), wide(prm[4])
    total[...] = jnp.zeros((COLS, NZ), F32)

    def sweep(t, _):
        inner = jnp.where(jnp.logical_and(t >= 2, t < CELLS // 8 - 2), 1.0, 0.0)
        odd = lax.rem(t, 2).astype(F32)
        added = None
        for j0 in range(0, 8, 2):
            pair = []
            for j in (j0, j0 + 1):
                r = 8 * t + j
                s = before[r]
                s = s + omega * ((resid[r] + spread(field, cz, t, j)) * rdiag[r] - s)
                part[r] = s
                f = root * s
                n = resid[r] - twice * s
                put_columns(fscr, (t, j), f)
                put_columns(nscr, (t, j), n)
                n = n * n
                if j == 0:
                    n = n * odd
                if j == 7:
                    n = n * (1.0 - odd)
                added = n if added is None else added + n
                pair.append(f)
            low[pl.ds(pl.multiple_of(64 * t + 8 * j0, 16), 16), :] = jnp.concatenate(pair, axis=0).astype(BF16)
        total[...] += inner * added
        return 0

    lax.fori_loop(0, CELLS // 8, sweep, 0)


def fix_faces(field, rdiag, cs, halos, scale):
    fb, fd, fc, fa = face_sides()
    rb, rd, rc, ra = halos

    def add(r, k, halo):
        v = coef(cs, k, r) * halo
        t, j = spot(r)
        v = v * rdiag[8 * t + j]
        if scale is not None:
            v = v * scale
        field[8 * t + j] += v

    tb, ta = jnp.where(fb, CELLS // 8 - 2, 0), jnp.where(fa, CELLS // 8 - 2, 0)
    kb, kd, kc, ka = jnp.where(fb, 1, 0), jnp.where(fd, 3, 2), jnp.where(fc, 3, 2), jnp.where(fa, 1, 0)
    for half in range(2):
        for j in range(8):
            add((tb + half, j), kb, rb[half * 8 + j])
            add((ta + half, j), ka, ra[half * 8 + j])

    def ys(i, _):
        add(y_row(fd, i), kd, rd[i])
        add(y_row(fc, i), kc, rc[i])
        return 0

    lax.fori_loop(0, LX, ys, 0, unroll=4)


def fix_kernel(which, old, rdiag, cs, prm, rb, rd, rc, ra, field, sb, sd, sc, sa):
    del old
    fix_faces(field, rdiag, cs, (rb, rd, rc, ra), wide(prm[which]) if which else None)
    fb, fd, fc, fa = face_sides()
    sb[...] = field[pl.ds(x_row(fb, 0), LY)]
    sa[...] = field[pl.ds(x_row(fa, 0), LY)]
    for i in range(LX):
        sd[i] = field[y_row(fd, i)]
        sc[i] = field[y_row(fc, i)]


def last_kernel(
    old, old_f, old_n, old_low, inner, rdiag, resid, cs, prm, rb, rd, rc, ra, ov,
    field, fscr, nscr, low, fac_hbm, new_hbm, msg, gq, sem,
):
    del old, old_f, old_n, old_low
    fix_faces(field, rdiag, cs, (rb, rd, rc, ra), wide(prm[2]))
    root, twice = wide(prm[3]), wide(prm[4])

    def finish(t, j0, counted):
        pair, added = [], None
        for j in (j0, j0 + 1):
            s = field[8 * t + j]
            f = root * s
            n = resid[8 * t + j] - twice * s
            put_columns(fscr, (t, j), f)
            put_columns(nscr, (t, j), n)
            if j in counted:
                added = n * n if added is None else added + n * n
            pair.append(f)
        low[pl.ds(pl.multiple_of(64 * t + 8 * j0, 16), 16), :] = jnp.concatenate(pair, axis=0).astype(BF16)
        return added

    total = inner[...]
    for t in (0, 1, CELLS // 8 - 2, CELLS // 8 - 1):
        for j0 in range(0, 8, 2):
            total = total + finish(t, j0, (j0, j0 + 1))

    def sides(x, total):
        return total + finish(2 * x, 0, (0,)) + finish(2 * x + 1, 6, (7,))

    total = lax.fori_loop(1, LX - 1, sides, total, unroll=2)
    put_f = pltpu.make_async_copy(fscr, fac_hbm, sem.at[0])
    put_n = pltpu.make_async_copy(nscr, new_hbm, sem.at[1])
    put_f.start()
    put_n.start()
    block = 64

    def gram(q, _):
        q0 = q * block
        p = None
        for x in range(LX):
            o = ov[pl.ds(q0, block), x].reshape(block * LY, NZ)
            w = low[x * 128 : x * 128 + 128, :]
            d = lax.dot_general(o, w, (((1,), (1,)), ((), ())), preferred_element_type=F32)
            p = d if p is None else p + d
        p = p.reshape(block, LY, 128)
        ysub = lax.broadcasted_iota(jnp.int32, (LY, 128), 0)
        ylane = lax.broadcasted_iota(jnp.int32, (LY, 128), 1) // COLS
        g = jnp.sum(jnp.where((ysub == ylane)[None], p, 0.0), axis=1)
        for shift in (64, 32, 16, 8):
            g = g + pltpu.roll(g, shift, 1)
        gq[pl.ds(pl.multiple_of(q0, block), block), :] = g
        return 0

    lax.fori_loop(0, QCOLS // block, gram, 0)
    g = jnp.transpose(gq[...])
    for c in range(COLS):
        msg[0:1, c * 128 : c * 128 + 128] = g[c : c + 1, :]
    squares = jnp.broadcast_to(jnp.sum(total, axis=1, keepdims=True), (COLS, 128))
    row = lax.broadcasted_iota(jnp.int32, (COLS, 128), 0)
    lane = lax.broadcasted_iota(jnp.int32, (COLS, 128), 1)
    msg[0:1, COLS * 128 :] = jnp.sum(jnp.where(row == lane, squares, 0.0), axis=0, keepdims=True)
    put_f.wait()
    put_n.wait()


def sum_kernel(parts, gram, norms):
    total = jnp.sum(parts[...], axis=0)
    for c in range(COLS):
        gram[c : c + 1, :] = total[:, c * 128 : c * 128 + 128]
    norms[...] = total[:, COLS * 128 :] / (CELLS * NZ * 128)


LIMIT = pltpu.CompilerParams(vmem_limit_bytes=8 << 20)
SENDS = (sds(XFACE), sds(YFACE), sds(YFACE), sds(XFACE))
ROWS = sds((COLS * STEP, 128))
COEFS = sds((6 * STEP, 128))


def in_hbm(x):
    return pltpu.with_memory_space_constraint(x, pltpu.HBM)


def pairs(n, first):
    out = []
    for i in range(first, n, 2):
        out += [(i, (i + 1) % n), ((i + 1) % n, i)]
    return out


def exchange(sends):
    sb, sd, sc, sa = sends
    rb = lax.ppermute(sb, GX, pairs(16, 1))
    rd = lax.ppermute(sd, GY, pairs(8, 1))
    rc = lax.ppermute(sc, GY, pairs(8, 0))
    ra = lax.ppermute(sa, GX, pairs(16, 0))
    return rb, rd, rc, ra


def local(resid_factor, coefficients, observer, shift_index):
    *sends, prm, rs, cs = pl.pallas_call(
        first_kernel, out_shape=(*SENDS, sds((5, COLS, 128)), ROWS, COEFS), in_specs=[SM, HB, HB], out_specs=(VM,) * 7,
        scratch_shapes=[pltpu.SemaphoreType.DMA((2,))], compiler_params=LIMIT, name="first",
    )(shift_index, in_hbm(stored(resid_factor)), in_hbm(stored(coefficients)))
    halos = exchange(sends)
    start, rdiag, resid, cz, part, seen = pl.pallas_call(
        second_kernel,
        out_shape=(sds(FIELD), sds(FIELD), sds(FIELD), COEFS, sds(FIELD), sds(observer.shape, BF16)),
        in_specs=[VM, VM, VM, HB], out_specs=(VM,) * 6, scratch_shapes=[pltpu.SemaphoreType.DMA],
        compiler_params=LIMIT, name="bulk_second",
    )(rs, cs, prm, in_hbm(observer))

    def fixed(which, part, halos):
        return pl.pallas_call(
            lambda *refs: fix_kernel(which, *refs), out_shape=(sds(FIELD), *SENDS), in_specs=[VM] * 8, out_specs=(VM,) * 5,
            input_output_aliases={0: 0}, compiler_params=LIMIT, name=f"fix_{which}",
        )(part, rdiag, cs, prm, *halos)

    second, *sends = fixed(0, part, halos)
    halos = exchange(sends)
    part = pl.pallas_call(
        third_kernel, out_shape=sds(FIELD), in_specs=[VM] * 6, out_specs=VM, compiler_params=LIMIT, name="bulk_third",
    )(second, start, resid, rdiag, cz, prm)
    third, *sends = fixed(1, part, halos)
    halos = exchange(sends)
    low = sds((COLS * CELLS, NZ), BF16)
    part, fscr, nscr, low_part, inner = pl.pallas_call(
        fourth_kernel, out_shape=(sds(FIELD), ROWS, ROWS, low, sds((COLS, NZ))), in_specs=[VM] * 6, out_specs=(VM,) * 5,
        compiler_params=LIMIT, name="bulk_fourth",
    )(third, second, resid, rdiag, cz, prm)
    *_, fac, new, msg = pl.pallas_call(
        last_kernel,
        out_shape=(sds(FIELD), ROWS, ROWS, low, ROWS, ROWS, sds((1, 9 * 128))),
        in_specs=[VM] * 14, out_specs=(VM, VM, VM, VM, HB, HB, VM), input_output_aliases={0: 0, 1: 1, 2: 2, 3: 3},
        scratch_shapes=[pltpu.VMEM((QCOLS, 128), F32), pltpu.SemaphoreType.DMA((2,))],
        compiler_params=LIMIT, name="last",
    )(part, fscr, nscr, low_part, inner, rdiag, resid, cs, prm, *halos, seen)
    msg = msg + lax.ppermute(msg, "core", [(0, 1), (1, 0)])
    gathered = lax.all_to_all(jnp.broadcast_to(msg, (64,) + msg.shape), CHIPS, 0, 0)
    gram, norms = pl.pallas_call(
        sum_kernel, out_shape=(sds((COLS, 128)), sds((1, 128))), in_specs=[VM], out_specs=(VM, VM), name="total",
    )(gathered)
    return unstored(fac), unstored(new), gram, norms[0, :COLS]


def solution(mesh):
    shape = (2, 4, 2, 2, 4)
    fine = Mesh(mesh.devices.reshape(shape), ("zh", "y", "core", "zl", "x"))
    placed = P(None, GX, GY, None)
    return jax.shard_map(
        local, mesh=fine, in_specs=(placed, placed, placed, P()), out_specs=(placed, placed, P(), P()), check_vma=False
    )
```

```python
import jax
import jax.numpy as jnp
from jax import lax
from jax.experimental import pallas as pl
from jax.experimental.pallas import tpu as pltpu
from jax.sharding import Mesh, PartitionSpec as P


COLS = 8
QCOLS = 128
LX = 8
LY = 16
CELLS = LX * LY
NZ = 512
ZT = NZ // 128
STEP = CELLS * ZT
F32 = jnp.float32
BF16 = jnp.bfloat16

GX = ("zh", "y", "core")
GY = ("zl", "x")
CHIPS = ("zh", "y", "zl", "x")

VM = pl.BlockSpec(memory_space=pltpu.VMEM)
HB = pl.BlockSpec(memory_space=pltpu.HBM)
SM = pl.BlockSpec(memory_space=pltpu.SMEM)

FIELD = (CELLS, COLS, NZ)
XFACE = (LY, COLS, NZ)
YFACE = (LX, COLS, NZ)


def sds(shape, dtype=F32):
    return jax.ShapeDtypeStruct(shape, dtype)


def stored(block):
    n = block.shape[0]
    return block.reshape(n, LX, LY // 8, 8, ZT, 128).transpose(0, 1, 2, 4, 3, 5).reshape(n * STEP, 128)


def unstored(rows):
    n = rows.shape[0] // STEP
    return rows.reshape(n, LX, LY // 8, ZT, 8, 128).transpose(0, 1, 2, 4, 3, 5).reshape(n, LX, LY, NZ)


def spot(r):
    return r if isinstance(r, tuple) else (r // 8, lax.rem(r, 8))


def coef(c_ref, k, r):
    t, j = spot(r)
    at = k * STEP + t * 32 + j
    return jnp.concatenate([c_ref[pl.ds(at + zt * 8, COLS, stride=0), :] for zt in range(ZT)], axis=1)


def columns(r_ref, r):
    t, j = spot(r)
    at = t * 32 + j
    return jnp.concatenate([r_ref[pl.ds(at + zt * 8, COLS, stride=STEP), :] for zt in range(ZT)], axis=1)


def put_columns(o_ref, r, v):
    t, j = spot(r)
    at = t * 32 + j
    for zt in range(ZT):
        o_ref[pl.ds(at + zt * 8, COLS, stride=STEP), :] = v[:, zt * 128 : zt * 128 + 128]


def swapped(vs):
    vs = list(vs)
    row = lax.broadcasted_iota(jnp.int32, vs[0].shape, 0)
    for step in (4, 2, 1):
        low = jnp.bitwise_and(row, step) == 0
        for i in range(8):
            if not i & step:
                a, b = vs[i], vs[i + step]
                vs[i] = jnp.where(low, a, pltpu.roll(b, step, 0))
                vs[i + step] = jnp.where(low, pltpu.roll(a, 8 - step, 0), b)
    return vs


def natural(r_ref, c, t):
    at = c * STEP + t * 32
    return jnp.concatenate([r_ref[pl.ds(at + zt * 8, 8), :] for zt in range(ZT)], axis=1)


def put_natural(o_ref, c, t, v):
    at = c * STEP + t * 32
    for zt in range(ZT):
        o_ref[pl.ds(at + zt * 8, 8), :] = v[:, zt * 128 : zt * 128 + 128]


def group(r_ref, t):
    return swapped([natural(r_ref, c, t) for c in range(COLS)])


def wide(v):
    return jnp.concatenate([v] * ZT, axis=1)


def x_row(high, i):
    return jnp.where(high, CELLS - LY, 0) + i


def y_row(high, i):
    return jnp.where(high, LY - 1, 0) + LY * i


def face_sides():
    even_x = lax.axis_index("core") == 0
    even_y = lax.rem(lax.axis_index("x"), 2) == 0
    return jnp.logical_not(even_x), jnp.logical_not(even_y), even_y, even_x


def first_kernel(shift_hbm, r_hbm, c_hbm, sb, sd, sc, sa, prm, rs, cs, shift_ref, sem):
    get_s = pltpu.make_async_copy(shift_hbm, shift_ref, sem.at[42])
    get_s.start()
    edge, inside = [], []
    for n, (far, near, count) in enumerate(((c_hbm, cs, 6), (r_hbm, rs, COLS))):
        for k in range(count):
            for part, (first, rows) in enumerate(((0, 64), (STEP - 64, 64), (64, STEP - 128))):
                at = pl.ds(k * STEP + first, rows)
                copy = pltpu.make_async_copy(far.at[at], near.at[at], sem.at[n * 18 + k * 3 + part])
                (inside if part == 2 else edge).append(copy)
    for copy in edge + inside:
        copy.start()
    get_s.wait()
    row = lax.broadcasted_iota(jnp.int32, (COLS, 128), 0)
    index = jnp.zeros((COLS, 128), F32)
    for c in range(COLS):
        index = jnp.where(row == c, shift_ref[c].astype(F32), index)
    sigma = 0.2 * jnp.exp(jnp.log(jnp.full((COLS, 128), 40.0, F32)) * index / 15.0)
    radius = 12.0 / (12.0 + sigma)
    omega_two = 1.0 / (1.0 - radius * radius / 2.0)
    omega_three = 1.0 / (1.0 - radius * radius * omega_two / 4.0)
    prm[0] = sigma
    prm[1] = omega_two
    prm[2] = omega_three
    prm[3] = jnp.sqrt(2.0 * sigma)
    prm[4] = 2.0 * sigma
    fb, fd, fc, fa = face_sides()
    sigma = wide(sigma)

    def diag_of(r):
        d = coef(cs, 0, r)
        for k in range(1, 6):
            d = d + coef(cs, k, r)
        return d + sigma

    tb, ta = jnp.where(fb, CELLS // 8 - 2, 0), jnp.where(fa, CELLS // 8 - 2, 0)
    for copy in edge:
        copy.wait()
    for half in range(2):
        for out, t in ((sb, tb + half), (sa, ta + half)):
            res = group(rs, t)
            for j in range(8):
                out[half * 8 + j] = res[j] / diag_of((t, j))
    for copy in inside:
        copy.wait()

    def ys(i, _):
        for out, r in ((sd, y_row(fd, i)), (sc, y_row(fc, i))):
            out[i] = columns(rs, r) / diag_of(r)
        return 0

    lax.fori_loop(0, LX, ys, 0, unroll=4)


def couplings(f_ref, cz, t):
    before, v = f_ref[jnp.maximum(8 * t - 1, 0)], f_ref[8 * t]
    for j in range(8):
        after = f_ref[jnp.minimum(8 * t + 8, CELLS - 1) if j == 7 else 8 * t + j + 1]
        total = coef(cz, 4, (t, j)) * pltpu.roll(v, 1, 1)
        total += coef(cz, 5, (t, j)) * pltpu.roll(v, NZ - 1, 1)
        total += coef(cz, 0, (t, j)) * f_ref[8 * jnp.maximum(t - 2, 0) + j]
        total += coef(cz, 1, (t, j)) * f_ref[8 * jnp.minimum(t + 2, CELLS // 8 - 1) + j]
        total += coef(cz, 2, (t, j)) * before
        total += coef(cz, 3, (t, j)) * after
        yield j, 8 * t + j, v, total
        before, v = v, after


def second_kernel(rs, cs, prm, o_hbm, start, rdiag, cz, part, ov, sem):
    load = pltpu.make_async_copy(o_hbm, ov, sem)
    load.start()
    sigma = wide(prm[0])
    row = lax.broadcasted_iota(jnp.int32, (64, 128), 0)
    lane = lax.broadcasted_iota(jnp.int32, (64, 128), 1)
    in32, in8 = lax.rem(row, 32), lax.rem(row, 8)
    outside = (
        None,
        None,
        jnp.logical_and(row < 32, in8 == 0),
        jnp.logical_and(row >= 32, in8 == 7),
        jnp.logical_and(in32 < 8, lane == 0),
        jnp.logical_and(in32 >= 24, lane == 127),
    )
    for k in range(6):
        for x in range(LX):
            rows = pl.ds(k * STEP + x * 64, 64)
            if (k, x) in ((0, 0), (1, LX - 1)):
                cz[rows, :] = jnp.zeros((64, 128), F32)
            elif k < 2:
                cz[rows, :] = cs[rows, :]
            else:
                cz[rows, :] = jnp.where(outside[k], 0.0, cs[rows, :])

    def begin(t, _):
        res = group(rs, t)
        for j in range(8):
            d = coef(cs, 0, (t, j))
            for k in range(1, 6):
                d = d + coef(cs, k, (t, j))
            recip = 1.0 / (d + sigma)
            rdiag[8 * t + j] = recip
            start[8 * t + j] = res[j] * recip
        return 0

    lax.fori_loop(0, CELLS // 8, begin, 0)

    def sweep(t, _):
        for _, r, v, total in couplings(start, cz, t):
            part[r] = v + total * rdiag[r]
        return 0

    lax.fori_loop(0, CELLS // 8, sweep, 0)
    load.wait()


def third_kernel(field, start, rdiag, cz, prm, part):
    omega = wide(prm[1])

    def sweep(t, _):
        for _, r, _, total in couplings(field, cz, t):
            part[r] = start[r] + omega * (total * rdiag[r])
        return 0

    lax.fori_loop(0, CELLS // 8, sweep, 0)


def splat(prm, k, c):
    return jnp.broadcast_to(wide(prm[k, c : c + 1, :]), (8, NZ))


def write_out(solved, rs, prm, fscr, nscr, t):
    for c, s in enumerate(swapped(solved)):
        put_natural(fscr, c, t, splat(prm, 3, c) * s)
        put_natural(nscr, c, t, natural(rs, c, t) - splat(prm, 4, c) * s)


def fourth_kernel(field, second, start, rdiag, rs, cz, prm, part, fscr, nscr, low):
    omega, root = wide(prm[2]), wide(prm[3])

    def sweep(t, _):
        solved = []
        for j, r, _, total in couplings(field, cz, t):
            s = second[r]
            s = s + omega * ((start[r] + total * rdiag[r]) - s)
            part[r] = s
            solved.append(s)
            if j % 2:
                pair = jnp.concatenate([root * solved[j - 1], root * s], axis=0)
                low[pl.ds(pl.multiple_of(64 * t + 8 * (j - 1), 16), 16), :] = pair.astype(BF16)
        write_out(solved, rs, prm, fscr, nscr, t)
        return 0

    lax.fori_loop(0, CELLS // 8, sweep, 0)


def fix_faces(field, rdiag, cs, halos, scale):
    fb, fd, fc, fa = face_sides()
    rb, rd, rc, ra = halos

    def add(r, k, halo):
        v = coef(cs, k, r) * halo
        t, j = spot(r)
        v = v * rdiag[8 * t + j]
        if scale is not None:
            v = v * scale
        field[8 * t + j] += v

    tb, ta = jnp.where(fb, CELLS // 8 - 2, 0), jnp.where(fa, CELLS // 8 - 2, 0)
    kb, kd, kc, ka = jnp.where(fb, 1, 0), jnp.where(fd, 3, 2), jnp.where(fc, 3, 2), jnp.where(fa, 1, 0)
    for half in range(2):
        for j in range(8):
            add((tb + half, j), kb, rb[half * 8 + j])
            add((ta + half, j), ka, ra[half * 8 + j])

    def ys(i, _):
        add(y_row(fd, i), kd, rd[i])
        add(y_row(fc, i), kc, rc[i])
        return 0

    lax.fori_loop(0, LX, ys, 0, unroll=4)


def fix_kernel(which, old, rdiag, cs, prm, rb, rd, rc, ra, field, sb, sd, sc, sa):
    del old
    fix_faces(field, rdiag, cs, (rb, rd, rc, ra), wide(prm[which]) if which else None)
    fb, fd, fc, fa = face_sides()
    sb[...] = field[pl.ds(x_row(fb, 0), LY)]
    sa[...] = field[pl.ds(x_row(fa, 0), LY)]
    for i in range(LX):
        sd[i] = field[y_row(fd, i)]
        sc[i] = field[y_row(fc, i)]


def last_kernel(
    old, old_f, old_n, old_low, rdiag, rs, cs, prm, rb, rd, rc, ra, ov,
    field, fscr, nscr, low, fac_hbm, new_hbm, msg, gq, sem,
):
    del old, old_f, old_n, old_low
    fix_faces(field, rdiag, cs, (rb, rd, rc, ra), wide(prm[2]))
    root, twice = wide(prm[3]), wide(prm[4])

    def put_low(t, j0):
        pair = jnp.concatenate([root * field[8 * t + j0], root * field[8 * t + j0 + 1]], axis=0)
        low[pl.ds(pl.multiple_of(64 * t + 8 * j0, 16), 16), :] = pair.astype(BF16)

    for t in (0, 1, CELLS // 8 - 2, CELLS // 8 - 1):
        write_out([field[8 * t + j] for j in range(8)], rs, prm, fscr, nscr, t)
        for j0 in range(0, 8, 2):
            put_low(t, j0)

    def sides(x, _):
        for t, j, j0 in ((2 * x, 0, 0), (2 * x + 1, 7, 6)):
            put_low(t, j0)
            s = field[8 * t + j]
            put_columns(fscr, (t, j), root * s)
            put_columns(nscr, (t, j), columns(rs, (t, j)) - twice * s)
        return 0

    lax.fori_loop(1, LX - 1, sides, 0, unroll=2)
    put_f = pltpu.make_async_copy(fscr, fac_hbm, sem.at[0])
    put_n = pltpu.make_async_copy(nscr, new_hbm, sem.at[1])
    put_f.start()
    put_n.start()
    block = 128

    def gram(q, _):
        q0 = q * block
        p = None
        for x in range(LX):
            o = ov[pl.ds(q0, block), x].reshape(block * LY, NZ)
            w = low[x * 128 : x * 128 + 128, :]
            d = lax.dot_general(o, w, (((1,), (1,)), ((), ())), preferred_element_type=F32)
            p = d if p is None else p + d
        p = p.reshape(block, LY, 128)
        ysub = lax.broadcasted_iota(jnp.int32, (LY, 128), 0)
        ylane = lax.broadcasted_iota(jnp.int32, (LY, 128), 1) // COLS
        g = jnp.sum(jnp.where((ysub == ylane)[None], p, 0.0), axis=1)
        for shift in (64, 32, 16, 8):
            g = g + pltpu.roll(g, shift, 1)
        gq[pl.ds(pl.multiple_of(q0, block), block), :] = g
        return 0

    lax.fori_loop(0, QCOLS // block, gram, 0)
    g = jnp.transpose(gq[...])
    for c in range(COLS):
        msg[0:1, c * 128 : c * 128 + 128] = g[c : c + 1, :]
    lane = lax.broadcasted_iota(jnp.int32, (1, 128), 1)
    norms = jnp.zeros((1, 128), F32)
    for c in range(COLS):
        parts = [jnp.zeros((8, 128), F32)] * 4
        for i in range(STEP // 8):
            n = nscr[c * STEP + i * 8 : c * STEP + i * 8 + 8, :]
            parts[i % 4] = parts[i % 4] + n * n
        total = jnp.sum(parts[0] + parts[1] + parts[2] + parts[3])
        norms = jnp.where(lane == c, total, norms)
    msg[0:1, COLS * 128 :] = norms
    put_f.wait()
    put_n.wait()


def sum_kernel(parts, gram, norms):
    total = jnp.sum(parts[...], axis=0)
    for c in range(COLS):
        gram[c : c + 1, :] = total[:, c * 128 : c * 128 + 128]
    norms[...] = (total[:, COLS * 128 : COLS * 128 + COLS] / (CELLS * NZ * 128)).reshape(COLS)


LIMIT = pltpu.CompilerParams(vmem_limit_bytes=8 << 20)
SENDS = (sds(XFACE), sds(YFACE), sds(YFACE), sds(XFACE))
ROWS = sds((COLS * STEP, 128))
COEFS = sds((6 * STEP, 128))


def in_hbm(x):
    return pltpu.with_memory_space_constraint(x, pltpu.HBM)


def pairs(n, first):
    out = []
    for i in range(first, n, 2):
        out += [(i, (i + 1) % n), ((i + 1) % n, i)]
    return out


def exchange(sends):
    sb, sd, sc, sa = sends
    rb = lax.ppermute(sb, GX, pairs(16, 1))
    rd = lax.ppermute(sd, GY, pairs(8, 1))
    rc = lax.ppermute(sc, GY, pairs(8, 0))
    ra = lax.ppermute(sa, GX, pairs(16, 0))
    return rb, rd, rc, ra


def local(resid_factor, coefficients, observer, shift_index):
    *sends, prm, rs, cs = pl.pallas_call(
        first_kernel, out_shape=(*SENDS, sds((5, COLS, 128)), ROWS, COEFS), in_specs=[HB] * 3, out_specs=(VM,) * 7,
        scratch_shapes=[pltpu.SMEM((COLS,), jnp.int32), pltpu.SemaphoreType.DMA((43,))], compiler_params=LIMIT, name="first",
    )(in_hbm(shift_index), in_hbm(stored(resid_factor)), in_hbm(stored(coefficients)))
    halos = exchange(sends)
    start, rdiag, cz, part, seen = pl.pallas_call(
        second_kernel,
        out_shape=(sds(FIELD), sds(FIELD), COEFS, sds(FIELD), sds(observer.shape, BF16)),
        in_specs=[VM, VM, VM, HB], out_specs=(VM,) * 5, scratch_shapes=[pltpu.SemaphoreType.DMA],
        compiler_params=LIMIT, name="bulk_second",
    )(rs, cs, prm, in_hbm(observer))

    def fixed(which, part, halos):
        return pl.pallas_call(
            lambda *refs: fix_kernel(which, *refs), out_shape=(sds(FIELD), *SENDS), in_specs=[VM] * 8, out_specs=(VM,) * 5,
            input_output_aliases={0: 0}, compiler_params=LIMIT,
        )(part, rdiag, cs, prm, *halos)

    second, *sends = fixed(0, part, halos)
    halos = exchange(sends)
    part = pl.pallas_call(
        third_kernel, out_shape=sds(FIELD), in_specs=[VM] * 5, out_specs=VM, compiler_params=LIMIT, name="bulk_third",
    )(second, start, rdiag, cz, prm)
    third, *sends = fixed(1, part, halos)
    halos = exchange(sends)
    low = sds((COLS * CELLS, NZ), BF16)
    part, fscr, nscr, low_part = pl.pallas_call(
        fourth_kernel, out_shape=(sds(FIELD), ROWS, ROWS, low), in_specs=[VM] * 7, out_specs=(VM,) * 4,
        compiler_params=LIMIT, name="bulk_fourth",
    )(third, second, start, rdiag, rs, cz, prm)
    *_, fac, new, msg = pl.pallas_call(
        last_kernel,
        out_shape=(sds(FIELD), ROWS, ROWS, low, ROWS, ROWS, sds((1, 9 * 128))),
        in_specs=[VM] * 13, out_specs=(VM, VM, VM, VM, HB, HB, VM), input_output_aliases={0: 0, 1: 1, 2: 2, 3: 3},
        scratch_shapes=[pltpu.VMEM((QCOLS, 128), F32), pltpu.SemaphoreType.DMA((2,))],
        compiler_params=LIMIT, name="last",
    )(part, fscr, nscr, low_part, rdiag, rs, cs, prm, *halos, seen)
    msg = msg + lax.ppermute(msg, "core", [(0, 1), (1, 0)])
    gathered = lax.all_to_all(jnp.broadcast_to(msg, (64,) + msg.shape), CHIPS, 0, 0)
    gram, norms = pl.pallas_call(
        sum_kernel, out_shape=(sds((COLS, 128)), sds((COLS,))), in_specs=[VM], out_specs=(VM, VM), name="total",
    )(pltpu.with_memory_space_constraint(gathered, pltpu.VMEM))
    return unstored(fac), unstored(new), gram, norms


def solution(mesh):
    shape = (2, 4, 2, 2, 4)
    fine = Mesh(mesh.devices.reshape(shape), ("zh", "y", "core", "zl", "x"))
    placed = P(None, GX, GY, None)
    return jax.shard_map(
        local, mesh=fine, in_specs=(placed, placed, placed, P()), out_specs=(placed, placed, P(), P()), check_vma=False
    )
```

```python
import jax
import jax.numpy as jnp
from jax import lax
from jax.experimental import pallas as pl
from jax.experimental.pallas import tpu as pltpu
from jax.sharding import Mesh, PartitionSpec as P


COLS = 8
QCOLS = 128
LX = 8
LY = 16
CELLS = LX * LY
NZ = 512
ZT = NZ // 128
STEP = CELLS * ZT
F32 = jnp.float32
BF16 = jnp.bfloat16

GX = ("zh", "y", "core")
GY = ("zl", "x")
CHIPS = ("zh", "y", "zl", "x")

VM = pl.BlockSpec(memory_space=pltpu.VMEM)
HB = pl.BlockSpec(memory_space=pltpu.HBM)
SM = pl.BlockSpec(memory_space=pltpu.SMEM)

FIELD = (CELLS, COLS, NZ)
XFACE = (LY, COLS, NZ)
YFACE = (LX, COLS, NZ)


def sds(shape, dtype=F32):
    return jax.ShapeDtypeStruct(shape, dtype)


def stored(block):
    n = block.shape[0]
    return block.reshape(n, LX, LY // 8, 8, ZT, 128).transpose(0, 1, 2, 4, 3, 5).reshape(n * STEP, 128)


def unstored(rows):
    n = rows.shape[0] // STEP
    return rows.reshape(n, LX, LY // 8, ZT, 8, 128).transpose(0, 1, 2, 4, 3, 5).reshape(n, LX, LY, NZ)


def spot(r):
    return r if isinstance(r, tuple) else (r // 8, lax.rem(r, 8))


def coef(c_ref, k, r):
    t, j = spot(r)
    at = k * STEP + t * 32 + j
    return jnp.concatenate([c_ref[pl.ds(at + zt * 8, COLS, stride=0), :] for zt in range(ZT)], axis=1)


def columns(r_ref, r):
    t, j = spot(r)
    at = t * 32 + j
    return jnp.concatenate([r_ref[pl.ds(at + zt * 8, COLS, stride=STEP), :] for zt in range(ZT)], axis=1)


def put_columns(o_ref, r, v):
    t, j = spot(r)
    at = t * 32 + j
    for zt in range(ZT):
        o_ref[pl.ds(at + zt * 8, COLS, stride=STEP), :] = v[:, zt * 128 : zt * 128 + 128]


def swapped(vs):
    vs = list(vs)
    row = lax.broadcasted_iota(jnp.int32, vs[0].shape, 0)
    for step in (4, 2, 1):
        low = jnp.bitwise_and(row, step) == 0
        for i in range(8):
            if not i & step:
                a, b = vs[i], vs[i + step]
                vs[i] = jnp.where(low, a, pltpu.roll(b, step, 0))
                vs[i + step] = jnp.where(low, pltpu.roll(a, 8 - step, 0), b)
    return vs


def natural(r_ref, c, t):
    at = c * STEP + t * 32
    return jnp.concatenate([r_ref[pl.ds(at + zt * 8, 8), :] for zt in range(ZT)], axis=1)


def put_natural(o_ref, c, t, v):
    at = c * STEP + t * 32
    for zt in range(ZT):
        o_ref[pl.ds(at + zt * 8, 8), :] = v[:, zt * 128 : zt * 128 + 128]


def group(r_ref, t):
    return swapped([natural(r_ref, c, t) for c in range(COLS)])


def wide(v):
    return jnp.concatenate([v] * ZT, axis=1)


def x_row(high, i):
    return jnp.where(high, CELLS - LY, 0) + i


def y_row(high, i):
    return jnp.where(high, LY - 1, 0) + LY * i


def face_sides():
    even_x = lax.axis_index("core") == 0
    even_y = lax.rem(lax.axis_index("x"), 2) == 0
    return jnp.logical_not(even_x), jnp.logical_not(even_y), even_y, even_x


def sum_of(cs, r):
    d = coef(cs, 0, r)
    for k in range(1, 6):
        d = d + coef(cs, k, r)
    return d


def first_kernel(shift_hbm, r_hbm, c_hbm, sb, sa, prm, rs, cs, shift_ref, sem):
    get_s = pltpu.make_async_copy(shift_hbm, shift_ref, sem.at[42])
    get_s.start()
    edge, inside = [], []
    for n, (far, near, count) in enumerate(((c_hbm, cs, 6), (r_hbm, rs, COLS))):
        for k in range(count):
            for part, (first, rows) in enumerate(((0, 64), (STEP - 64, 64), (64, STEP - 128))):
                at = pl.ds(k * STEP + first, rows)
                copy = pltpu.make_async_copy(far.at[at], near.at[at], sem.at[n * 18 + k * 3 + part])
                (inside if part == 2 else edge).append(copy)
    for copy in edge + inside:
        copy.start()
    get_s.wait()
    row = lax.broadcasted_iota(jnp.int32, (COLS, 128), 0)
    index = jnp.zeros((COLS, 128), F32)
    for c in range(COLS):
        index = jnp.where(row == c, shift_ref[c].astype(F32), index)
    sigma = 0.2 * jnp.exp(jnp.log(jnp.full((COLS, 128), 40.0, F32)) * index / 15.0)
    radius = 12.0 / (12.0 + sigma)
    omega_two = 1.0 / (1.0 - radius * radius / 2.0)
    omega_three = 1.0 / (1.0 - radius * radius * omega_two / 4.0)
    prm[0] = sigma
    prm[1] = omega_two
    prm[2] = omega_three
    prm[3] = jnp.sqrt(2.0 * sigma)
    prm[4] = 2.0 * sigma
    fb, _, _, fa = face_sides()
    sigma = wide(sigma)
    tb, ta = jnp.where(fb, CELLS // 8 - 2, 0), jnp.where(fa, CELLS // 8 - 2, 0)
    for copy in edge:
        copy.wait()
    for half in range(2):
        for out, t in ((sb, tb + half), (sa, ta + half)):
            res = group(rs, t)
            for j in range(8):
                out[half * 8 + j] = res[j] / (sum_of(cs, (t, j)) + sigma)
    for copy in inside:
        copy.wait()


def first_sides_kernel(rs, cs, prm, sd, sc):
    _, fd, fc, _ = face_sides()
    sigma = wide(prm[0])

    def ys(i, _):
        for out, r in ((sd, y_row(fd, i)), (sc, y_row(fc, i))):
            out[i] = columns(rs, r) / (sum_of(cs, r) + sigma)
        return 0

    lax.fori_loop(0, LX, ys, 0, unroll=4)


def couplings(f_ref, cz, t):
    before, v = f_ref[jnp.maximum(8 * t - 1, 0)], f_ref[8 * t]
    for j in range(8):
        after = f_ref[jnp.minimum(8 * t + 8, CELLS - 1) if j == 7 else 8 * t + j + 1]
        total = coef(cz, 4, (t, j)) * pltpu.roll(v, 1, 1)
        total += coef(cz, 5, (t, j)) * pltpu.roll(v, NZ - 1, 1)
        total += coef(cz, 0, (t, j)) * f_ref[8 * jnp.maximum(t - 2, 0) + j]
        total += coef(cz, 1, (t, j)) * f_ref[8 * jnp.minimum(t + 2, CELLS // 8 - 1) + j]
        total += coef(cz, 2, (t, j)) * before
        total += coef(cz, 3, (t, j)) * after
        yield j, 8 * t + j, v, total
        before, v = v, after


def second_kernel(rs, cs, prm, o_hbm, start, rdiag, cz, part, ov, sem):
    load = pltpu.make_async_copy(o_hbm, ov, sem)
    load.start()
    sigma = wide(prm[0])
    row = lax.broadcasted_iota(jnp.int32, (64, 128), 0)
    lane = lax.broadcasted_iota(jnp.int32, (64, 128), 1)
    in32, in8 = lax.rem(row, 32), lax.rem(row, 8)
    outside = (
        None,
        None,
        jnp.logical_and(row < 32, in8 == 0),
        jnp.logical_and(row >= 32, in8 == 7),
        jnp.logical_and(in32 < 8, lane == 0),
        jnp.logical_and(in32 >= 24, lane == 127),
    )
    for k in range(6):
        for x in range(LX):
            rows = pl.ds(k * STEP + x * 64, 64)
            if (k, x) in ((0, 0), (1, LX - 1)):
                cz[rows, :] = jnp.zeros((64, 128), F32)
            elif k < 2:
                cz[rows, :] = cs[rows, :]
            else:
                cz[rows, :] = jnp.where(outside[k], 0.0, cs[rows, :])

    def begin(t, _):
        res = group(rs, t)
        for j in range(8):
            d = coef(cs, 0, (t, j))
            for k in range(1, 6):
                d = d + coef(cs, k, (t, j))
            recip = 1.0 / (d + sigma)
            rdiag[8 * t + j] = recip
            start[8 * t + j] = res[j] * recip
        return 0

    lax.fori_loop(0, CELLS // 8, begin, 0)

    def sweep(t, _):
        for _, r, v, total in couplings(start, cz, t):
            part[r] = v + total * rdiag[r]
        return 0

    lax.fori_loop(0, CELLS // 8, sweep, 0)
    load.wait()


def third_kernel(field, start, rdiag, cz, prm, part):
    omega = wide(prm[1])

    def sweep(t, _):
        for _, r, _, total in couplings(field, cz, t):
            part[r] = start[r] + omega * (total * rdiag[r])
        return 0

    lax.fori_loop(0, CELLS // 8, sweep, 0)


def splat(prm, k, c):
    return jnp.broadcast_to(wide(prm[k, c : c + 1, :]), (8, NZ))


def write_out(solved, rs, prm, fscr, nscr, t):
    for c, s in enumerate(swapped(solved)):
        put_natural(fscr, c, t, splat(prm, 3, c) * s)
        put_natural(nscr, c, t, natural(rs, c, t) - splat(prm, 4, c) * s)


def fourth_kernel(field, second, start, rdiag, rs, cz, prm, part, fscr, nscr, low):
    omega, root = wide(prm[2]), wide(prm[3])

    def sweep(t, _):
        solved = []
        for j, r, _, total in couplings(field, cz, t):
            s = second[r]
            s = s + omega * ((start[r] + total * rdiag[r]) - s)
            part[r] = s
            solved.append(s)
            if j % 2:
                pair = jnp.concatenate([root * solved[j - 1], root * s], axis=0)
                low[pl.ds(pl.multiple_of(64 * t + 8 * (j - 1), 16), 16), :] = pair.astype(BF16)
        write_out(solved, rs, prm, fscr, nscr, t)
        return 0

    lax.fori_loop(0, CELLS // 8, sweep, 0)


def fix_faces(field, rdiag, cs, halos, scale):
    fb, fd, fc, fa = face_sides()
    rb, rd, rc, ra = halos

    def add(r, k, halo):
        v = coef(cs, k, r) * halo
        t, j = spot(r)
        v = v * rdiag[8 * t + j]
        if scale is not None:
            v = v * scale
        field[8 * t + j] += v

    tb, ta = jnp.where(fb, CELLS // 8 - 2, 0), jnp.where(fa, CELLS // 8 - 2, 0)
    kb, kd, kc, ka = jnp.where(fb, 1, 0), jnp.where(fd, 3, 2), jnp.where(fc, 3, 2), jnp.where(fa, 1, 0)
    for half in range(2):
        for j in range(8):
            add((tb + half, j), kb, rb[half * 8 + j])
            add((ta + half, j), ka, ra[half * 8 + j])

    def ys(i, _):
        add(y_row(fd, i), kd, rd[i])
        add(y_row(fc, i), kc, rc[i])
        return 0

    lax.fori_loop(0, LX, ys, 0, unroll=4)


def fix_kernel(which, old, rdiag, cs, prm, rb, rd, rc, ra, field, sb, sd, sc, sa):
    del old
    fix_faces(field, rdiag, cs, (rb, rd, rc, ra), wide(prm[which]) if which else None)
    fb, fd, fc, fa = face_sides()
    sb[...] = field[pl.ds(x_row(fb, 0), LY)]
    sa[...] = field[pl.ds(x_row(fa, 0), LY)]
    for i in range(LX):
        sd[i] = field[y_row(fd, i)]
        sc[i] = field[y_row(fc, i)]


def last_kernel(
    old, old_f, old_n, old_low, rdiag, rs, cs, prm, rb, rd, rc, ra, ov,
    field, fscr, nscr, low, fac_hbm, new_hbm, msg, gq, sem,
):
    del old, old_f, old_n, old_low
    fix_faces(field, rdiag, cs, (rb, rd, rc, ra), wide(prm[2]))
    root, twice = wide(prm[3]), wide(prm[4])

    def put_low(t, j0):
        pair = jnp.concatenate([root * field[8 * t + j0], root * field[8 * t + j0 + 1]], axis=0)
        low[pl.ds(pl.multiple_of(64 * t + 8 * j0, 16), 16), :] = pair.astype(BF16)

    for t in (0, 1, CELLS // 8 - 2, CELLS // 8 - 1):
        write_out([field[8 * t + j] for j in range(8)], rs, prm, fscr, nscr, t)
        for j0 in range(0, 8, 2):
            put_low(t, j0)

    def sides(x, _):
        for t, j, j0 in ((2 * x, 0, 0), (2 * x + 1, 7, 6)):
            put_low(t, j0)
            s = field[8 * t + j]
            put_columns(fscr, (t, j), root * s)
            put_columns(nscr, (t, j), columns(rs, (t, j)) - twice * s)
        return 0

    lax.fori_loop(1, LX - 1, sides, 0, unroll=2)
    put_f = pltpu.make_async_copy(fscr, fac_hbm, sem.at[0])
    put_n = pltpu.make_async_copy(nscr, new_hbm, sem.at[1])
    put_f.start()
    put_n.start()
    block = 128

    def gram(q, _):
        q0 = q * block
        p = None
        for x in range(LX):
            o = ov[pl.ds(q0, block), x].reshape(block * LY, NZ)
            w = low[x * 128 : x * 128 + 128, :]
            d = lax.dot_general(o, w, (((1,), (1,)), ((), ())), preferred_element_type=F32)
            p = d if p is None else p + d
        p = p.reshape(block, LY, 128)
        ysub = lax.broadcasted_iota(jnp.int32, (LY, 128), 0)
        ylane = lax.broadcasted_iota(jnp.int32, (LY, 128), 1) // COLS
        g = jnp.sum(jnp.where((ysub == ylane)[None], p, 0.0), axis=1)
        for shift in (64, 32, 16, 8):
            g = g + pltpu.roll(g, shift, 1)
        gq[pl.ds(pl.multiple_of(q0, block), block), :] = g
        return 0

    lax.fori_loop(0, QCOLS // block, gram, 0)
    g = jnp.transpose(gq[...])
    for c in range(COLS):
        msg[0:1, c * 128 : c * 128 + 128] = g[c : c + 1, :]
    lane = lax.broadcasted_iota(jnp.int32, (1, 128), 1)
    norms = jnp.zeros((1, 128), F32)
    for c in range(COLS):
        parts = [jnp.zeros((8, 128), F32)] * 4
        for i in range(STEP // 8):
            n = nscr[c * STEP + i * 8 : c * STEP + i * 8 + 8, :]
            parts[i % 4] = parts[i % 4] + n * n
        total = jnp.sum(parts[0] + parts[1] + parts[2] + parts[3])
        norms = jnp.where(lane == c, total, norms)
    msg[0:1, COLS * 128 :] = norms
    put_f.wait()
    put_n.wait()


def sum_kernel(parts, gram, norms):
    total = jnp.sum(parts[...], axis=0)
    for c in range(COLS):
        gram[c : c + 1, :] = total[:, c * 128 : c * 128 + 128]
    norms[...] = (total[:, COLS * 128 : COLS * 128 + COLS] / (CELLS * NZ * 128)).reshape(COLS)


LIMIT = pltpu.CompilerParams(vmem_limit_bytes=8 << 20)
SENDS = (sds(XFACE), sds(YFACE), sds(YFACE), sds(XFACE))
ROWS = sds((COLS * STEP, 128))
COEFS = sds((6 * STEP, 128))


def in_hbm(x):
    return pltpu.with_memory_space_constraint(x, pltpu.HBM)


def pairs(n, first):
    out = []
    for i in range(first, n, 2):
        out += [(i, (i + 1) % n), ((i + 1) % n, i)]
    return out


def exchange(sends):
    sb, sd, sc, sa = sends
    rb = lax.ppermute(sb, GX, pairs(16, 1))
    rd = lax.ppermute(sd, GY, pairs(8, 1))
    rc = lax.ppermute(sc, GY, pairs(8, 0))
    ra = lax.ppermute(sa, GX, pairs(16, 0))
    return rb, rd, rc, ra


def local(resid_factor, coefficients, observer, shift_index):
    sb, sa, prm, rs, cs = pl.pallas_call(
        first_kernel, out_shape=(sds(XFACE), sds(XFACE), sds((5, COLS, 128)), ROWS, COEFS), in_specs=[HB] * 3, out_specs=(VM,) * 5,
        scratch_shapes=[pltpu.SMEM((COLS,), jnp.int32), pltpu.SemaphoreType.DMA((43,))], compiler_params=LIMIT, name="first",
    )(in_hbm(shift_index), in_hbm(stored(resid_factor)), in_hbm(stored(coefficients)))
    sd, sc = pl.pallas_call(
        first_sides_kernel, out_shape=(sds(YFACE), sds(YFACE)), in_specs=[VM] * 3, out_specs=(VM, VM),
        compiler_params=LIMIT, name="sides",
    )(rs, cs, prm)
    sends = (sb, sd, sc, sa)
    halos = exchange(sends)
    start, rdiag, cz, part, seen = pl.pallas_call(
        second_kernel,
        out_shape=(sds(FIELD), sds(FIELD), COEFS, sds(FIELD), sds(observer.shape, BF16)),
        in_specs=[VM, VM, VM, HB], out_specs=(VM,) * 5, scratch_shapes=[pltpu.SemaphoreType.DMA],
        compiler_params=LIMIT, name="bulk_second",
    )(rs, cs, prm, in_hbm(observer))

    def fixed(which, part, halos):
        return pl.pallas_call(
            lambda *refs: fix_kernel(which, *refs), out_shape=(sds(FIELD), *SENDS), in_specs=[VM] * 8, out_specs=(VM,) * 5,
            input_output_aliases={0: 0}, compiler_params=LIMIT,
        )(part, rdiag, cs, prm, *halos)

    second, *sends = fixed(0, part, halos)
    halos = exchange(sends)
    part = pl.pallas_call(
        third_kernel, out_shape=sds(FIELD), in_specs=[VM] * 5, out_specs=VM, compiler_params=LIMIT, name="bulk_third",
    )(second, start, rdiag, cz, prm)
    third, *sends = fixed(1, part, halos)
    halos = exchange(sends)
    low = sds((COLS * CELLS, NZ), BF16)
    part, fscr, nscr, low_part = pl.pallas_call(
        fourth_kernel, out_shape=(sds(FIELD), ROWS, ROWS, low), in_specs=[VM] * 7, out_specs=(VM,) * 4,
        compiler_params=LIMIT, name="bulk_fourth",
    )(third, second, start, rdiag, rs, cz, prm)
    *_, fac, new, msg = pl.pallas_call(
        last_kernel,
        out_shape=(sds(FIELD), ROWS, ROWS, low, ROWS, ROWS, sds((1, 9 * 128))),
        in_specs=[VM] * 13, out_specs=(VM, VM, VM, VM, HB, HB, VM), input_output_aliases={0: 0, 1: 1, 2: 2, 3: 3},
        scratch_shapes=[pltpu.VMEM((QCOLS, 128), F32), pltpu.SemaphoreType.DMA((2,))],
        compiler_params=LIMIT, name="last",
    )(part, fscr, nscr, low_part, rdiag, rs, cs, prm, *halos, seen)
    msg = msg + lax.ppermute(msg, "core", [(0, 1), (1, 0)])
    gathered = lax.all_to_all(jnp.broadcast_to(msg, (64,) + msg.shape), CHIPS, 0, 0)
    gram, norms = pl.pallas_call(
        sum_kernel, out_shape=(sds((COLS, 128)), sds((COLS,))), in_specs=[VM], out_specs=(VM, VM), name="total",
    )(pltpu.with_memory_space_constraint(gathered, pltpu.VMEM))
    return unstored(fac), unstored(new), gram, norms


def solution(mesh):
    shape = (2, 4, 2, 2, 4)
    fine = Mesh(mesh.devices.reshape(shape), ("zh", "y", "core", "zl", "x"))
    placed = P(None, GX, GY, None)
    return jax.shard_map(
        local, mesh=fine, in_specs=(placed, placed, placed, P()), out_specs=(placed, placed, P(), P()), check_vma=False
    )
```
